32 devices in a mesh: row: 4 (over y, core), col: 8 (over z, x).
Axes of the slice: x: 2, y: 2, z: 4, core: 2. Of those that a mesh axis runs over, the one named last changes fastest.
Arguments:
- b_tensor: bfloat16 [128, 1024, 1024], P('col', 'row'), may hold values from -6 to 6
- occ_green: bfloat16 [1024, 1024], P(('row', 'col')), may hold values from -0.1875 to 0.1875
- virt_green: bfloat16 [1024, 1024], P(('row', 'col')), may hold values from -0.1875 to 0.1875
- b_mask: int32 [1, 8, 8], replicated, may hold values 0 or 1
- occ_mask: int32 [8, 8], replicated, may hold values 0 or 1
- virt_mask: int32 [8, 8], replicated, may hold values 0 or 1
Outputs:
- chi: float32 [128, 128], P(('row', 'col'))
The draws below stay inside these ranges and needn't reach their ends.
All inputs are finite; a program needn't handle non-finite values.
Results may differ from the reference program's by a relative error of at most 0.0041.
Values may be sent and summed in bfloat16 or wider, within the bound.
No kernel may reach another device: no remote copies, remote signals or barrier semaphores. Data moves between devices by JAX's collectives and lax.ppermute only.
A program may use at most 128 MiB of HBM per device.

```python
import jax
import jax.numpy as jnp
from jax import lax

TILE = 128
AO_TILES = 8
RI_TILES = 1
NAO = 1024
NP = 128


def touch_ends(array, stream_key, low, largest):
    spot = [jax.random.randint(jax.random.fold_in(stream_key, axis), (), 0, length) for axis, length in enumerate(array.shape)]
    longest = array.shape.index(max(array.shape))
    neighbour = spot[:longest] + [(spot[longest] + 1) % array.shape[longest]] + spot[longest + 1:]
    return array.at[tuple(spot)].set(low).at[tuple(neighbour)].set(largest)


def steps_of(stream_key, extent, split, least, top_value):
    def one(axis_at, parts):
        steps = jax.random.uniform(jax.random.fold_in(jax.random.fold_in(stream_key, 6), axis_at), (parts,), jnp.float32, least / len(split), top_value / len(split))
        return jnp.repeat(jnp.exp(steps), extent[axis_at] // parts).reshape((-1,) + (1,) * (len(extent) - axis_at - 1))

    loudness = one(*split[0])
    for cut in split[1:]:
        loudness = loudness * one(*cut)
    return loudness


def centred(rng, dims, scale, reach, split=(), dtype=jnp.bfloat16):
    result = jax.random.normal(rng, dims, jnp.float32) * scale
    if len(split) > 0:
        result = steps_of(rng, dims, split, -0.22, 0.18) * result
    return jnp.clip(result, min=-reach, max=reach).astype(dtype)


def setup_inputs(seed: int = 0) -> dict:
    streams_of = jax.random.split(jax.random.key(seed), 7)
    b_tensor = centred(streams_of[0], (NP, NAO, NAO), 1.0, 6.0, ((0, 8), (1, 4)))
    occ_green = centred(streams_of[1], (NAO, NAO), NAO ** -0.5, 0.1875, ((0, 32),))
    virt_green = centred(streams_of[2], (NAO, NAO), NAO ** -0.5, 0.1875, ((0, 32),))
    b_mask = touch_ends((jax.random.randint(streams_of[3], (RI_TILES, AO_TILES, AO_TILES), 0, 4) < 3).astype(jnp.int32), jax.random.fold_in(streams_of[3], 1), 0, 1)
    occ_mask = touch_ends((jax.random.randint(streams_of[4], (AO_TILES, AO_TILES), 0, 4) < 3).astype(jnp.int32), jax.random.fold_in(streams_of[4], 1), 0, 1)
    virt_mask = touch_ends((jax.random.randint(streams_of[5], (AO_TILES, AO_TILES), 0, 4) < 3).astype(jnp.int32), jax.random.fold_in(streams_of[5], 1), 0, 1)
    return dict(b_tensor=b_tensor, occ_green=occ_green, virt_green=virt_green, b_mask=b_mask, occ_mask=occ_mask, virt_mask=virt_mask)


def expand_pair(mask):
    return jnp.repeat(jnp.repeat(mask, TILE, axis=0), TILE, axis=1).astype(jnp.bfloat16)


def reference(b_tensor, occ_green, virt_green, b_mask, occ_mask, virt_mask):
    occ = occ_green * expand_pair(occ_mask)
    virt = virt_green * expand_pair(virt_mask)
    blocks = b_tensor.reshape(RI_TILES, TILE, NAO, NAO)

    def one_tile(items):
        block, mask = items
        masked = block * expand_pair(mask)[None]
        half = jnp.dot(masked.reshape(-1, NAO), virt, preferred_element_type=jnp.float32)
        half = half.astype(jnp.bfloat16).reshape(TILE, NAO, NAO)
        full = jnp.einsum("lm,pms->pls", occ.astype(jnp.float32), half.astype(jnp.float32))
        return full.astype(jnp.bfloat16), masked

    full_all, masked_all = lax.map(one_tile, (blocks, b_mask))
    total = jnp.dot(full_all.reshape(NP, -1), masked_all.reshape(NP, -1).T, preferred_element_type=jnp.float32)
    return total * (-2.0 / NAO)
```

```python
import functools

import jax
import jax.numpy as jnp
from jax import lax
from jax.experimental import pallas as pl
from jax.experimental.pallas import tpu as pltpu
from jax.sharding import PartitionSpec as P


CHUNKS = 4


def chunk_sizes(count):
    last = max(1, count // 8)
    parts = CHUNKS - 1
    return [(count - last + parts - 1 - i) // parts for i in range(parts)] + [last]


def xor_bits(size):
    bits = []
    bit = size // 2
    while bit:
        bits.append(bit)
        bit //= 2
    return bits


def gather_bits(size):
    bits = xor_bits(size)
    return bits[-1:] + bits[:-1]


def swap(value, axis, size, bit):
    return lax.ppermute(value, axis, [(i, i ^ bit) for i in range(size)])


def join(held, other, upper, axis):
    return jnp.stack(
        [jnp.where(upper, other, held), jnp.where(upper, held, other)], axis=axis
    )


def plan_kernel(row_size, p_tiles, caps, me, mask_ref, tile_ref, on_ref, branch_ref):
    tiles, across = mask_ref.shape[1:]
    m_tiles = tiles // row_size
    slots = m_tiles * across

    def used(row, slot):
        found = 0
        for p in range(p_tiles):
            found |= mask_ref[p, row * m_tiles + slot // across, slot % across]
        return (found != 0).astype(jnp.int32)

    most = 0
    for row in range(row_size):
        most = jnp.maximum(most, sum(used(row, slot) for slot in range(slots)))
    branch_ref[0] = sum((most > cap).astype(jnp.int32) for cap in caps[:-1])
    front = 0
    back = sum(used(me[1], slot) for slot in range(slots))
    for slot in range(slots):
        here = used(me[1], slot)
        at = jnp.where(here != 0, front, back)
        tile_ref[at] = slot
        on_ref[at] = mask_ref[me[2], me[1] * m_tiles + slot // across, slot % across]
        front += here
        back += 1 - here


def plan(b_mask, me, row_size, caps):
    p_tiles, tiles, across = b_mask.shape
    slots = tiles // row_size * across
    small = pl.BlockSpec(memory_space=pltpu.SMEM)
    return pl.pallas_call(
        functools.partial(plan_kernel, row_size, p_tiles, caps),
        out_shape=[jax.ShapeDtypeStruct((size,), jnp.int32) for size in (slots, slots, 1)],
        in_specs=[small, small],
        out_specs=[small] * 3,
    )(me, b_mask)


def pack_kernel(near, slots, tile, across, me, slot_tile, slot_on, b_ref, *refs):
    out_refs, wide = refs[:-1], refs[-1]
    wide[...] = b_ref[0].astype(jnp.float32)
    cols = len(out_refs) if near else out_refs[0].shape[0]
    rows = tile // cols

    @pl.loop(0, slots)
    def _(slot):
        top = (slot_tile[slot] // across) * tile
        lane = pl.multiple_of((slot_tile[slot] % across) * tile, tile)
        for k in range(cols):
            start = top + ((me[0] ^ k) if near else k) * rows
            block = wide[pl.ds(pl.multiple_of(start, rows), rows), pl.ds(lane, tile)]
            block = jnp.where(slot_on[slot] != 0, block, 0.0).astype(b_ref.dtype)
            if near:
                out_refs[k][slot, 0] = block
            else:
                out_refs[0][k, slot, 0] = block


def pack(b, first, count, near, me, slot_tile, slot_on, cols, tile):
    _, m_count, n_basis = b.shape
    slots = slot_tile.shape[0]
    rows = tile // cols
    if near:
        out_shape = [jax.ShapeDtypeStruct((slots, count, rows, tile), b.dtype)] * cols
        out_specs = [pl.BlockSpec((slots, 1, rows, tile), lambda p, *_: (0, p, 0, 0))] * cols
    else:
        out_shape = [jax.ShapeDtypeStruct((cols, slots, count, rows, tile), b.dtype)]
        out_specs = [pl.BlockSpec((cols, slots, 1, rows, tile), lambda p, *_: (0, 0, p, 0, 0))]
    return pl.pallas_call(
        functools.partial(pack_kernel, near, slots, tile, n_basis // tile),
        out_shape=out_shape,
        grid_spec=pltpu.PrefetchScalarGridSpec(
            num_scalar_prefetch=3,
            grid=(count,),
            in_specs=[pl.BlockSpec((1, m_count, n_basis), lambda p, *_: (p + first, 0, 0))],
            out_specs=out_specs,
            scratch_shapes=[pltpu.VMEM((m_count, n_basis), jnp.float32)],
        ),
    )(me, slot_tile, slot_on, b)


def lane_block(n_basis):
    return min(256, n_basis)


def keep_tiles(mask_ref, first, tile, value_ref, out_ref):
    rows, lanes = out_ref.shape

    @pl.loop(0, rows // tile)
    def _(i):
        down = pl.ds(pl.multiple_of(i * tile, tile), tile)
        for j in range(lanes // tile):
            at = (down, slice(j * tile, (j + 1) * tile))
            kept = value_ref[at]
            out_ref[at] = jnp.where(mask_ref[first + i, j] != 0, kept, jnp.zeros_like(kept))


def mask_kernel(tile, first, mask_ref, value_ref, out_ref):
    keep_tiles(mask_ref, first[0], tile, value_ref, out_ref)


def masked_tiles(value, mask, first, tile):
    return pl.pallas_call(
        functools.partial(mask_kernel, tile),
        out_shape=jax.ShapeDtypeStruct(value.shape, value.dtype),
        grid_spec=pltpu.PrefetchScalarGridSpec(
            num_scalar_prefetch=2,
            grid=(),
            in_specs=[pl.BlockSpec(memory_space=pltpu.VMEM)],
            out_specs=pl.BlockSpec(memory_space=pltpu.VMEM),
        ),
    )(jnp.reshape(first, (1,)), mask, value)


def inner_kernel(tile, starts, sizes, mask_ref, b_ref, virt_ref, *refs):
    out_refs, masked = refs[:-1], refs[-1]
    keep_tiles(mask_ref, 0, tile, b_ref.at[0], masked)
    n_basis = masked.shape[1]
    width = lane_block(n_basis)
    p = pl.program_id(0)

    @pl.loop(0, n_basis // width)
    def _(j):
        lanes = pl.ds(pl.multiple_of(j * width, width), width)
        part = jnp.dot(
            masked[...], virt_ref[:, lanes], preferred_element_type=jnp.float32
        ).astype(masked.dtype)
        for start, size, out_ref in zip(starts, sizes, out_refs):

            @pl.when((p >= start) & (p < start + size))
            def _():
                out_ref[0, :, lanes] = part


def inner(b, first, sizes, mask, virt, tile):
    _, rows, n_basis = b.shape
    starts = [sum(sizes[:i]) for i in range(len(sizes))]
    return pl.pallas_call(
        functools.partial(inner_kernel, tile, starts, sizes),
        out_shape=[jax.ShapeDtypeStruct((size, rows, n_basis), b.dtype) for size in sizes],
        grid_spec=pltpu.PrefetchScalarGridSpec(
            num_scalar_prefetch=1,
            grid=(sum(sizes),),
            in_specs=[
                pl.BlockSpec((1, rows, n_basis), lambda p, mask: (p + first, 0, 0)),
                pl.BlockSpec((n_basis, n_basis), lambda p, mask: (0, 0)),
            ],
            out_specs=[
                pl.BlockSpec(
                    (1, rows, n_basis),
                    lambda p, mask, start=start, size=size: (
                        jnp.clip(p - start, 0, size - 1),
                        0,
                        0,
                    ),
                )
                for start, size in zip(starts, sizes)
            ],
            scratch_shapes=[pltpu.VMEM((rows, n_basis), b.dtype)],
        ),
    )(mask, b, virt)


def outer_kernel(offsets, slots, tile, across, me, slot_tile, occ_ref, *refs):
    half_refs = refs[: len(offsets)]
    out_refs, wide = refs[len(offsets) : -1], refs[-1]
    depth = half_refs[0].shape[1]
    rows = out_refs[0].shape[2]
    width = lane_block(wide.shape[1])

    @pl.loop(0, wide.shape[1] // width)
    def _(j):
        lanes = pl.ds(pl.multiple_of(j * width, width), width)
        total = None
        for offset, half_ref in zip(offsets, half_refs):
            start = pl.multiple_of((me[1] ^ offset) * depth, depth)
            part = jnp.dot(
                occ_ref[:, pl.ds(start, depth)],
                half_ref[0, :, lanes],
                preferred_element_type=jnp.float32,
            )
            total = part if total is None else total + part
        wide[:, lanes] = total

    @pl.loop(0, slots)
    def _(slot):
        top = (slot_tile[slot] // across) * tile
        lane = pl.multiple_of((slot_tile[slot] % across) * tile, tile)
        for k, out_ref in enumerate(out_refs):
            start = pl.multiple_of(top + (me[0] ^ k) * rows, rows)
            block = wide[pl.ds(start, rows), pl.ds(lane, tile)]
            out_ref[slot, 0] = block.astype(out_ref.dtype)


def outer(occ, halves, offsets, me, slot_tile, cols, tile):
    count, depth, n_basis = halves[0].shape
    slots = slot_tile.shape[0]
    strip = (slots, count, tile // cols, tile)
    return pl.pallas_call(
        functools.partial(outer_kernel, offsets, slots, tile, n_basis // tile),
        out_shape=[jax.ShapeDtypeStruct(strip, occ.dtype)] * cols,
        grid_spec=pltpu.PrefetchScalarGridSpec(
            num_scalar_prefetch=2,
            grid=(count,),
            in_specs=[pl.BlockSpec(occ.shape, lambda p, me, which: (0, 0))]
            + [pl.BlockSpec((1, depth, n_basis), lambda p, me, which: (p, 0, 0))] * len(halves),
            out_specs=[
                pl.BlockSpec((slots, 1) + strip[2:], lambda p, me, which: (0, p, 0, 0))
            ]
            * cols,
            scratch_shapes=[pltpu.VMEM((occ.shape[0], n_basis), jnp.float32)],
        ),
    )(me, slot_tile, occ, *halves)


def group_of(slots):
    groups = [size for size in range(2, 9) if slots % size == 0]
    return max(groups, default=slots)


def place(me, strips, slot, wide, base, stride):
    for k, ref in enumerate(strips):
        count = ref.shape[1]
        wide[pl.ds((me[0] ^ k) * stride + base, count)] = ref[slot].astype(jnp.float32)


def unroll_rows(wide, out_ref, start):
    turned = jnp.swapaxes(wide[...], 0, 1).astype(out_ref.dtype)
    rows, _, lanes = turned.shape
    for row in range(rows):
        at = start + row * lanes
        at = at if isinstance(at, int) else pl.multiple_of(at, lanes)
        out_ref[:, pl.ds(at, lanes)] = turned[row]


def flatten_kernel(group, early, me, *refs):
    near_refs, rest_ref, out_ref, wide = refs[:-3], refs[-3], refs[-2], refs[-1]
    cols, _, late, rows, lanes = rest_ref.shape

    @pl.loop(0, group)
    def _(slot):
        place(me, near_refs, slot, wide, 0, early + late)
        for k in range(cols):
            start = k * (early + late) + early
            wide[start : start + late] = rest_ref[k, slot].astype(jnp.float32)
        unroll_rows(wide, out_ref, slot * (rows * lanes))


def flatten(near, rest, me):
    cols, slots, late, rows, lanes = rest.shape
    early = near[0].shape[1]
    total = cols * (early + late)
    group = group_of(slots)
    return pl.pallas_call(
        functools.partial(flatten_kernel, group, early),
        out_shape=jax.ShapeDtypeStruct((total, slots * rows * lanes), rest.dtype),
        grid_spec=pltpu.PrefetchScalarGridSpec(
            num_scalar_prefetch=1,
            grid=(slots // group,),
            in_specs=[pl.BlockSpec((group, early, rows, lanes), lambda s, me: (s, 0, 0, 0))]
            * cols
            + [pl.BlockSpec((cols, group, late, rows, lanes), lambda s, me: (0, s, 0, 0, 0))],
            out_specs=pl.BlockSpec((total, group * rows * lanes), lambda s, me: (0, s)),
            scratch_shapes=[pltpu.VMEM((total, rows, lanes), jnp.float32)],
        ),
    )(me, *near, rest)


def contract_kernel(group, counts, cols, me, *refs):
    strips, b_ref, out_ref, wide, flat = refs[:-4], *refs[-4:]
    width = flat.shape[1]

    @pl.when(pl.program_id(0) == 0)
    def _():
        out_ref[...] = jnp.zeros_like(out_ref)

    @pl.loop(0, group)
    def _(slot):
        base = 0
        for i, count in enumerate(counts):
            place(me, strips[i * cols : (i + 1) * cols], slot, wide, base, sum(counts))
            base += count
        unroll_rows(wide, flat, 0)
        out_ref[...] += lax.dot_general(
            flat[...],
            b_ref[:, pl.ds(pl.multiple_of(slot * width, width), width)],
            (((1,), (1,)), ((), ())),
            preferred_element_type=jnp.float32,
        )


def contract(chunks, b_flat, me):
    cols = len(chunks[0])
    slots, _, rows, lanes = chunks[0][0].shape
    counts = [chunk[0].shape[1] for chunk in chunks]
    total, width = cols * sum(counts), rows * lanes
    group = group_of(slots)
    return pl.pallas_call(
        functools.partial(contract_kernel, group, counts, cols),
        out_shape=jax.ShapeDtypeStruct((total, b_flat.shape[0]), jnp.float32),
        grid_spec=pltpu.PrefetchScalarGridSpec(
            num_scalar_prefetch=1,
            grid=(slots // group,),
            in_specs=[
                pl.BlockSpec((group, count, rows, lanes), lambda s, me: (s, 0, 0, 0))
                for count in counts
                for _ in range(cols)
            ]
            + [pl.BlockSpec((b_flat.shape[0], group * width), lambda s, me: (0, s))],
            out_specs=pl.BlockSpec((total, b_flat.shape[0]), lambda s, me: (0, 0)),
            scratch_shapes=[
                pltpu.VMEM((total, rows, lanes), jnp.float32),
                pltpu.VMEM((total, width), b_flat.dtype),
            ],
        ),
    )(me, *[strip for chunk in chunks for strip in chunk], b_flat)


def exchange(strips):
    return [strips[0]] + [swap(s, "col", len(strips), k) for k, s in enumerate(strips) if k]


def per_device(row_size, col_size, b_tensor, occ_green, virt_green, b_mask, occ_mask, virt_mask):
    p_count, m_count, n_basis = b_tensor.shape
    tile = n_basis // b_mask.shape[2]
    col_index, row_index = lax.axis_index("col"), lax.axis_index("row")
    me = jnp.stack([col_index, row_index, (col_index * p_count) // tile]).astype(jnp.int32)
    caps = slot_caps(m_count // tile * (n_basis // tile))
    slot_tile, slot_on, branch = plan(b_mask, me, row_size, caps)

    def with_slots(cap, *args):
        return run(row_size, col_size, tile, slot_tile[:cap], slot_on[:cap], me, *args)

    return lax.switch(
        branch[0],
        [functools.partial(with_slots, cap) for cap in caps],
        b_tensor,
        occ_green,
        virt_green,
        b_mask,
        occ_mask,
        virt_mask,
    )


def slot_caps(slots):
    return sorted({slots * part // 16 for part in (13, 14, 16)})


def run(
    row_size,
    col_size,
    tile,
    slot_tile,
    slot_on,
    me,
    b_tensor,
    occ_green,
    virt_green,
    b_mask,
    occ_mask,
    virt_mask,
):
    col_index, row_index = me[0], me[1]
    p_count, m_count, n_basis = b_tensor.shape
    m_tiles = m_count // tile
    across = n_basis // tile
    local_mask = lax.dynamic_slice(b_mask, (me[2], row_index * m_tiles, 0), (1, m_tiles, across))[0]

    green, seen = jnp.stack([virt_green, occ_green]), []
    for bit in gather_bits(col_size):
        upper = (col_index & bit) != 0
        axis = 1 + sum(other > bit for other in seen)
        seen.append(bit)
        green = join(green, swap(green, "col", col_size, bit), upper, axis)
    virt_rows, occ_rows = green.reshape(2, -1, n_basis)

    early = max(1, p_count // 8)
    strips = pack(b_tensor, 0, early, True, me, slot_tile, slot_on, col_size, tile)
    near = exchange(strips)
    (strips,) = pack(
        b_tensor, early, p_count - early, False, me, slot_tile, slot_on, col_size, tile
    )
    rest = lax.all_to_all(strips, "col", split_axis=0, concat_axis=0, tiled=True)

    virt = virt_rows
    for depth, bit in enumerate(xor_bits(row_size)):
        upper = (row_index & bit) != 0
        virt = join(virt, swap(virt, "row", row_size, bit), upper, depth)
    virt = masked_tiles(virt.reshape(n_basis, n_basis), virt_mask, 0, tile)
    occ = masked_tiles(occ_rows, occ_mask, row_index * m_tiles, tile)

    sizes = chunk_sizes(p_count)
    offsets = [0]
    for bit in xor_bits(row_size):
        offsets = offsets + [offset ^ bit for offset in offsets]
    ready = inner(b_tensor, 0, sizes[:1], local_mask, virt, tile)
    ready += inner(b_tensor, sizes[0], sizes[1:], local_mask, virt, tile)
    gathered = []
    for k in range(CHUNKS):
        halves = [ready[k]]
        for bit in xor_bits(row_size):
            halves = halves + [swap(h, "row", row_size, bit) for h in halves]
        gathered.append(halves)
    moved = []
    for k in range(CHUNKS):
        strips = outer(occ, gathered[k], offsets, me, slot_tile, col_size, tile)
        moved.append(exchange(strips))

    b_flat = flatten(near, rest, me)
    sums = []
    sums.append(contract(moved[:-1], b_flat, me))
    sums.append(contract(moved[-1:], b_flat, me))
    sums = [part.reshape(col_size, -1, part.shape[-1]) for part in sums]
    total = jnp.concatenate(sums, axis=1)
    total = total.reshape(row_size * col_size, -1, total.shape[-1])
    shares = lax.all_to_all(total, ("row", "col"), split_axis=0, concat_axis=0, tiled=True)
    return shares.sum(0) * (-2.0 / n_basis)


def solution(mesh):
    row_size, col_size = mesh.shape["row"], mesh.shape["col"]

    return jax.shard_map(
        functools.partial(per_device, row_size, col_size),
        mesh=mesh,
        in_specs=(
            P("col", "row", None),
            P(("row", "col"), None),
            P(("row", "col"), None),
            P(),
            P(),
            P(),
        ),
        out_specs=P(("row", "col"), None),
        check_vma=False,
    )
```

```python
import functools

import jax
import jax.numpy as jnp
from jax import lax
from jax.experimental import pallas as pl
from jax.experimental.pallas import tpu as pltpu
from jax.sharding import PartitionSpec as P


CHUNKS = 4


def chunk_sizes(count):
    last = max(1, count // 8)
    parts = CHUNKS - 1
    return [(count - last + parts - 1 - i) // parts for i in range(parts)] + [last]


def xor_bits(size):
    bits = []
    bit = size // 2
    while bit:
        bits.append(bit)
        bit //= 2
    return bits


def swap(value, axis, size, bit):
    return lax.ppermute(value, axis, [(i, i ^ bit) for i in range(size)])


def join(held, other, upper, axis):
    return jnp.stack(
        [jnp.where(upper, other, held), jnp.where(upper, held, other)], axis=axis
    )


def plan_kernel(row_size, p_tiles, caps, me, mask_ref, tile_ref, on_ref, branch_ref):
    tiles, across = mask_ref.shape[1:]
    m_tiles = tiles // row_size
    slots = m_tiles * across

    def used(row, slot):
        found = 0
        for p in range(p_tiles):
            found |= mask_ref[p, row * m_tiles + slot // across, slot % across]
        return (found != 0).astype(jnp.int32)

    most = 0
    for row in range(row_size):
        most = jnp.maximum(most, sum(used(row, slot) for slot in range(slots)))
    branch_ref[0] = sum((most > cap).astype(jnp.int32) for cap in caps[:-1])
    front = 0
    back = sum(used(me[1], slot) for slot in range(slots))
    for slot in range(slots):
        here = used(me[1], slot)
        at = jnp.where(here != 0, front, back)
        tile_ref[at] = slot
        on_ref[at] = mask_ref[me[2], me[1] * m_tiles + slot // across, slot % across]
        front += here
        back += 1 - here


def plan(b_mask, me, row_size, caps):
    p_tiles, tiles, across = b_mask.shape
    slots = tiles // row_size * across
    small = pl.BlockSpec(memory_space=pltpu.SMEM)
    return pl.pallas_call(
        functools.partial(plan_kernel, row_size, p_tiles, caps),
        out_shape=[jax.ShapeDtypeStruct((size,), jnp.int32) for size in (slots, slots, 1)],
        in_specs=[small, small],
        out_specs=[small] * 3,
    )(me, b_mask)


def pack_kernel(near, slots, tile, across, me, slot_tile, slot_on, b_ref, *refs):
    out_refs, wide = refs[:-1], refs[-1]
    wide[...] = b_ref[0].astype(jnp.float32)
    cols = len(out_refs) if near else out_refs[0].shape[0]
    rows = tile // cols

    @pl.loop(0, slots)
    def _(slot):
        top = (slot_tile[slot] // across) * tile
        lane = pl.multiple_of((slot_tile[slot] % across) * tile, tile)
        for k in range(cols):
            start = top + ((me[0] ^ k) if near else k) * rows
            block = wide[pl.ds(pl.multiple_of(start, rows), rows), pl.ds(lane, tile)]
            block = jnp.where(slot_on[slot] != 0, block, 0.0).astype(b_ref.dtype)
            if near:
                out_refs[k][slot, 0] = block
            else:
                out_refs[0][k, slot, 0] = block


def pack(b, first, count, near, me, slot_tile, slot_on, cols, tile):
    _, m_count, n_basis = b.shape
    slots = slot_tile.shape[0]
    rows = tile // cols
    if near:
        out_shape = [jax.ShapeDtypeStruct((slots, count, rows, tile), b.dtype)] * cols
        out_specs = [pl.BlockSpec((slots, 1, rows, tile), lambda p, *_: (0, p, 0, 0))] * cols
    else:
        out_shape = [jax.ShapeDtypeStruct((cols, slots, count, rows, tile), b.dtype)]
        out_specs = [pl.BlockSpec((cols, slots, 1, rows, tile), lambda p, *_: (0, 0, p, 0, 0))]
    return pl.pallas_call(
        functools.partial(pack_kernel, near, slots, tile, n_basis // tile),
        out_shape=out_shape,
        grid_spec=pltpu.PrefetchScalarGridSpec(
            num_scalar_prefetch=3,
            grid=(count,),
            in_specs=[pl.BlockSpec((1, m_count, n_basis), lambda p, *_: (p + first, 0, 0))],
            out_specs=out_specs,
            scratch_shapes=[pltpu.VMEM((m_count, n_basis), jnp.float32)],
        ),
    )(me, slot_tile, slot_on, b)


def lane_block(n_basis, most):
    return min(most, n_basis)


def keep_tiles(mask_ref, first, tile, value_ref, out_ref):
    rows, lanes = out_ref.shape

    @pl.loop(0, rows // tile)
    def _(i):
        down = pl.ds(pl.multiple_of(i * tile, tile), tile)
        for j in range(lanes // tile):
            at = (down, slice(j * tile, (j + 1) * tile))
            kept = value_ref[at]
            out_ref[at] = jnp.where(mask_ref[first + i, j] != 0, kept, jnp.zeros_like(kept))


def mask_kernel(tile, first, mask_ref, value_ref, out_ref):
    keep_tiles(mask_ref, first[0], tile, value_ref, out_ref)


def masked_tiles(value, mask, first, tile):
    return pl.pallas_call(
        functools.partial(mask_kernel, tile),
        out_shape=jax.ShapeDtypeStruct(value.shape, value.dtype),
        grid_spec=pltpu.PrefetchScalarGridSpec(
            num_scalar_prefetch=2,
            grid=(),
            in_specs=[pl.BlockSpec(memory_space=pltpu.VMEM)],
            out_specs=pl.BlockSpec(memory_space=pltpu.VMEM),
        ),
    )(jnp.reshape(first, (1,)), mask, value)


def inner_kernel(tile, starts, sizes, mask_ref, b_ref, virt_ref, *refs):
    out_refs, masked = refs[:-1], refs[-1]
    keep_tiles(mask_ref, 0, tile, b_ref.at[0], masked)
    n_basis = masked.shape[1]
    width = lane_block(n_basis, 512)
    p = pl.program_id(0)

    @pl.loop(0, n_basis // width)
    def _(j):
        lanes = pl.ds(pl.multiple_of(j * width, width), width)
        part = jnp.dot(
            masked[...], virt_ref[:, lanes], preferred_element_type=jnp.float32
        ).astype(masked.dtype)
        for start, size, out_ref in zip(starts, sizes, out_refs):

            @pl.when((p >= start) & (p < start + size))
            def _():
                out_ref[0, :, lanes] = part


def inner(b, first, sizes, mask, virt, tile):
    _, rows, n_basis = b.shape
    starts = [sum(sizes[:i]) for i in range(len(sizes))]
    return pl.pallas_call(
        functools.partial(inner_kernel, tile, starts, sizes),
        out_shape=[jax.ShapeDtypeStruct((size, rows, n_basis), b.dtype) for size in sizes],
        grid_spec=pltpu.PrefetchScalarGridSpec(
            num_scalar_prefetch=1,
            grid=(sum(sizes),),
            in_specs=[
                pl.BlockSpec((1, rows, n_basis), lambda p, mask: (p + first, 0, 0)),
                pl.BlockSpec((n_basis, n_basis), lambda p, mask: (0, 0)),
            ],
            out_specs=[
                pl.BlockSpec(
                    (1, rows, n_basis),
                    lambda p, mask, start=start, size=size: (
                        jnp.clip(p - start, 0, size - 1),
                        0,
                        0,
                    ),
                )
                for start, size in zip(starts, sizes)
            ],
            scratch_shapes=[pltpu.VMEM((rows, n_basis), b.dtype)],
        ),
    )(mask, b, virt)


def outer_kernel(offsets, slots, tile, across, me, slot_tile, occ_ref, *refs):
    half_refs = refs[: len(offsets)]
    out_refs, wide = refs[len(offsets) : -1], refs[-1]
    depth = half_refs[0].shape[1]
    rows = out_refs[0].shape[2]
    width = lane_block(wide.shape[1], 256)

    @pl.loop(0, wide.shape[1] // width)
    def _(j):
        lanes = pl.ds(pl.multiple_of(j * width, width), width)
        total = None
        for offset, half_ref in zip(offsets, half_refs):
            start = pl.multiple_of((me[1] ^ offset) * depth, depth)
            part = jnp.dot(
                occ_ref[:, pl.ds(start, depth)],
                half_ref[0, :, lanes],
                preferred_element_type=jnp.float32,
            )
            total = part if total is None else total + part
        wide[:, lanes] = total

    @pl.loop(0, slots)
    def _(slot):
        top = (slot_tile[slot] // across) * tile
        lane = pl.multiple_of((slot_tile[slot] % across) * tile, tile)
        for k, out_ref in enumerate(out_refs):
            start = pl.multiple_of(top + (me[0] ^ k) * rows, rows)
            block = wide[pl.ds(start, rows), pl.ds(lane, tile)]
            out_ref[slot, 0] = block.astype(out_ref.dtype)


def outer(occ, halves, offsets, me, slot_tile, cols, tile):
    count, depth, n_basis = halves[0].shape
    slots = slot_tile.shape[0]
    strip = (slots, count, tile // cols, tile)
    return pl.pallas_call(
        functools.partial(outer_kernel, offsets, slots, tile, n_basis // tile),
        out_shape=[jax.ShapeDtypeStruct(strip, occ.dtype)] * cols,
        grid_spec=pltpu.PrefetchScalarGridSpec(
            num_scalar_prefetch=2,
            grid=(count,),
            in_specs=[pl.BlockSpec(occ.shape, lambda p, me, which: (0, 0))]
            + [pl.BlockSpec((1, depth, n_basis), lambda p, me, which: (p, 0, 0))] * len(halves),
            out_specs=[
                pl.BlockSpec((slots, 1) + strip[2:], lambda p, me, which: (0, p, 0, 0))
            ]
            * cols,
            scratch_shapes=[pltpu.VMEM((occ.shape[0], n_basis), jnp.float32)],
        ),
    )(me, slot_tile, occ, *halves)


def group_of(slots):
    groups = [size for size in range(2, 9) if slots % size == 0]
    return max(groups, default=slots)


def place(me, strips, slot, wide, base, stride):
    for k, ref in enumerate(strips):
        count = ref.shape[1]
        wide[pl.ds((me[0] ^ k) * stride + base, count)] = ref[slot].astype(jnp.float32)


def unroll_rows(wide, out_ref, start):
    turned = jnp.swapaxes(wide[...], 0, 1).astype(out_ref.dtype)
    rows, _, lanes = turned.shape
    for row in range(rows):
        at = start + row * lanes
        at = at if isinstance(at, int) else pl.multiple_of(at, lanes)
        out_ref[:, pl.ds(at, lanes)] = turned[row]


def flatten_kernel(group, early, me, *refs):
    near_refs, rest_ref, out_ref, wide = refs[:-3], refs[-3], refs[-2], refs[-1]
    cols, _, late, rows, lanes = rest_ref.shape

    @pl.loop(0, group)
    def _(slot):
        place(me, near_refs, slot, wide, 0, early + late)
        for k in range(cols):
            start = k * (early + late) + early
            wide[start : start + late] = rest_ref[k, slot].astype(jnp.float32)
        unroll_rows(wide, out_ref, slot * (rows * lanes))


def flatten(near, rest, me):
    cols, slots, late, rows, lanes = rest.shape
    early = near[0].shape[1]
    total = cols * (early + late)
    group = group_of(slots)
    return pl.pallas_call(
        functools.partial(flatten_kernel, group, early),
        out_shape=jax.ShapeDtypeStruct((total, slots * rows * lanes), rest.dtype),
        grid_spec=pltpu.PrefetchScalarGridSpec(
            num_scalar_prefetch=1,
            grid=(slots // group,),
            in_specs=[pl.BlockSpec((group, early, rows, lanes), lambda s, me: (s, 0, 0, 0))]
            * cols
            + [pl.BlockSpec((cols, group, late, rows, lanes), lambda s, me: (0, s, 0, 0, 0))],
            out_specs=pl.BlockSpec((total, group * rows * lanes), lambda s, me: (0, s)),
            scratch_shapes=[pltpu.VMEM((total, rows, lanes), jnp.float32)],
        ),
    )(me, *near, rest)


def contract_kernel(group, counts, cols, me, *refs):
    strips, b_ref, out_ref, wide, flat = refs[:-4], *refs[-4:]
    width = flat.shape[1]

    @pl.when(pl.program_id(0) == 0)
    def _():
        out_ref[...] = jnp.zeros_like(out_ref)

    @pl.loop(0, group)
    def _(slot):
        base = 0
        for i, count in enumerate(counts):
            place(me, strips[i * cols : (i + 1) * cols], slot, wide, base, sum(counts))
            base += count
        unroll_rows(wide, flat, 0)
        out_ref[...] += lax.dot_general(
            flat[...],
            b_ref[:, pl.ds(pl.multiple_of(slot * width, width), width)],
            (((1,), (1,)), ((), ())),
            preferred_element_type=jnp.float32,
        )


def contract(chunks, b_flat, me):
    cols = len(chunks[0])
    slots, _, rows, lanes = chunks[0][0].shape
    counts = [chunk[0].shape[1] for chunk in chunks]
    total, width = cols * sum(counts), rows * lanes
    group = group_of(slots)
    return pl.pallas_call(
        functools.partial(contract_kernel, group, counts, cols),
        out_shape=jax.ShapeDtypeStruct((total, b_flat.shape[0]), jnp.float32),
        grid_spec=pltpu.PrefetchScalarGridSpec(
            num_scalar_prefetch=1,
            grid=(slots // group,),
            in_specs=[
                pl.BlockSpec((group, count, rows, lanes), lambda s, me: (s, 0, 0, 0))
                for count in counts
                for _ in range(cols)
            ]
            + [pl.BlockSpec((b_flat.shape[0], group * width), lambda s, me: (0, s))],
            out_specs=pl.BlockSpec((total, b_flat.shape[0]), lambda s, me: (0, 0)),
            scratch_shapes=[
                pltpu.VMEM((total, rows, lanes), jnp.float32),
                pltpu.VMEM((total, width), b_flat.dtype),
            ],
        ),
    )(me, *[strip for chunk in chunks for strip in chunk], b_flat)


def exchange(strips):
    return [strips[0]] + [swap(s, "col", len(strips), k) for k, s in enumerate(strips) if k]


def per_device(row_size, col_size, b_tensor, occ_green, virt_green, b_mask, occ_mask, virt_mask):
    p_count, m_count, n_basis = b_tensor.shape
    tile = n_basis // b_mask.shape[2]
    col_index, row_index = lax.axis_index("col"), lax.axis_index("row")
    me = jnp.stack([col_index, row_index, (col_index * p_count) // tile]).astype(jnp.int32)
    caps = slot_caps(m_count // tile * (n_basis // tile))
    slot_tile, slot_on, branch = plan(b_mask, me, row_size, caps)

    def with_slots(cap, *args):
        return run(row_size, col_size, tile, slot_tile[:cap], slot_on[:cap], me, *args)

    return lax.switch(
        branch[0],
        [functools.partial(with_slots, cap) for cap in caps],
        b_tensor,
        occ_green,
        virt_green,
        b_mask,
        occ_mask,
        virt_mask,
    )


def slot_caps(slots):
    return sorted({slots * part // 16 for part in (13, 14, 16)})


def run(
    row_size,
    col_size,
    tile,
    slot_tile,
    slot_on,
    me,
    b_tensor,
    occ_green,
    virt_green,
    b_mask,
    occ_mask,
    virt_mask,
):
    col_index, row_index = me[0], me[1]
    p_count, m_count, n_basis = b_tensor.shape
    m_tiles = m_count // tile
    across = n_basis // tile
    local_mask = lax.dynamic_slice(b_mask, (me[2], row_index * m_tiles, 0), (1, m_tiles, across))[0]

    green, seen = jnp.stack([virt_green, occ_green]), []
    for bit in xor_bits(col_size):
        upper = (col_index & bit) != 0
        axis = 1 + sum(other > bit for other in seen)
        seen.append(bit)
        green = join(green, swap(green, "col", col_size, bit), upper, axis)
    virt_rows, occ_rows = green.reshape(2, -1, n_basis)

    early = max(1, p_count * 3 // 16)
    strips = pack(b_tensor, 0, early, True, me, slot_tile, slot_on, col_size, tile)
    near = exchange(strips)
    (strips,) = pack(
        b_tensor, early, p_count - early, False, me, slot_tile, slot_on, col_size, tile
    )
    rest = lax.all_to_all(strips, "col", split_axis=0, concat_axis=0, tiled=True)

    virt = virt_rows
    for depth, bit in enumerate(xor_bits(row_size)):
        upper = (row_index & bit) != 0
        virt = join(virt, swap(virt, "row", row_size, bit), upper, depth)
    virt = masked_tiles(virt.reshape(n_basis, n_basis), virt_mask, 0, tile)
    occ = masked_tiles(occ_rows, occ_mask, row_index * m_tiles, tile)

    sizes = chunk_sizes(p_count)
    offsets = [0]
    for bit in xor_bits(row_size):
        offsets = offsets + [offset ^ bit for offset in offsets]
    ready = inner(b_tensor, 0, sizes[:1], local_mask, virt, tile)
    ready += inner(b_tensor, sizes[0], sizes[1:], local_mask, virt, tile)
    gathered = []
    for k in range(CHUNKS):
        halves = [ready[k]]
        for bit in xor_bits(row_size):
            halves = halves + [swap(h, "row", row_size, bit) for h in halves]
        gathered.append(halves)
    moved = []
    for k in range(CHUNKS):
        strips = outer(occ, gathered[k], offsets, me, slot_tile, col_size, tile)
        moved.append(exchange(strips))

    b_flat = flatten(near, rest, me)
    sums = []
    sums.append(contract(moved[:-1], b_flat, me))
    sums.append(contract(moved[-1:], b_flat, me))
    sums = [part.reshape(col_size, -1, part.shape[-1]) for part in sums]
    total = jnp.concatenate(sums, axis=1)
    total = total.reshape(row_size * col_size, -1, total.shape[-1])
    shares = lax.all_to_all(total, ("row", "col"), split_axis=0, concat_axis=0, tiled=True)
    return shares.sum(0) * (-2.0 / n_basis)


def solution(mesh):
    row_size, col_size = mesh.shape["row"], mesh.shape["col"]

    return jax.shard_map(
        functools.partial(per_device, row_size, col_size),
        mesh=mesh,
        in_specs=(
            P("col", "row", None),
            P(("row", "col"), None),
            P(("row", "col"), None),
            P(),
            P(),
            P(),
        ),
        out_specs=P(("row", "col"), None),
        check_vma=False,
    )
```

```python
import functools

import jax
import jax.numpy as jnp
from jax import lax
from jax.experimental import pallas as pl
from jax.experimental.pallas import tpu as pltpu
from jax.sharding import PartitionSpec as P


CHUNKS = 4


def chunk_sizes(count):
    last = max(1, count // 8)
    parts = CHUNKS - 1
    return [(count - last + parts - 1 - i) // parts for i in range(parts)] + [last]


def xor_bits(size):
    bits = []
    bit = size // 2
    while bit:
        bits.append(bit)
        bit //= 2
    return bits


def swap(value, axis, size, bit):
    return lax.ppermute(value, axis, [(i, i ^ bit) for i in range(size)])


def join(held, other, upper, axis):
    return jnp.stack(
        [jnp.where(upper, other, held), jnp.where(upper, held, other)], axis=axis
    )


def plan_kernel(row_size, p_tiles, caps, me, mask_ref, tile_ref, on_ref, branch_ref):
    tiles, across = mask_ref.shape[1:]
    m_tiles = tiles // row_size
    slots = m_tiles * across

    def used(row, slot):
        found = 0
        for p in range(p_tiles):
            found |= mask_ref[p, row * m_tiles + slot // across, slot % across]
        return (found != 0).astype(jnp.int32)

    most = 0
    for row in range(row_size):
        most = jnp.maximum(most, sum(used(row, slot) for slot in range(slots)))
    branch_ref[0] = sum((most > cap).astype(jnp.int32) for cap in caps[:-1])
    front = 0
    back = sum(used(me[1], slot) for slot in range(slots))
    for slot in range(slots):
        here = used(me[1], slot)
        at = jnp.where(here != 0, front, back)
        tile_ref[at] = slot
        on_ref[at] = mask_ref[me[2], me[1] * m_tiles + slot // across, slot % across]
        front += here
        back += 1 - here


def plan(b_mask, me, row_size, caps):
    p_tiles, tiles, across = b_mask.shape
    slots = tiles // row_size * across
    small = pl.BlockSpec(memory_space=pltpu.SMEM)
    return pl.pallas_call(
        functools.partial(plan_kernel, row_size, p_tiles, caps),
        out_shape=[jax.ShapeDtypeStruct((size,), jnp.int32) for size in (slots, slots, 1)],
        in_specs=[small, small],
        out_specs=[small] * 3,
    )(me, b_mask)


def pack_kernel(near, slots, tile, across, me, slot_tile, slot_on, b_ref, *refs):
    out_refs, wide = refs[:-1], refs[-1]
    wide[...] = b_ref[0].astype(jnp.float32)
    cols = len(out_refs) if near else out_refs[0].shape[0]
    rows = tile // cols

    @pl.loop(0, slots)
    def _(slot):
        top = (slot_tile[slot] // across) * tile
        lane = pl.multiple_of((slot_tile[slot] % across) * tile, tile)
        for k in range(cols):
            start = top + ((me[0] ^ k) if near else k) * rows
            block = wide[pl.ds(pl.multiple_of(start, rows), rows), pl.ds(lane, tile)]
            block = jnp.where(slot_on[slot] != 0, block, 0.0).astype(b_ref.dtype)
            if near:
                out_refs[k][slot, 0] = block
            else:
                out_refs[0][k, slot, 0] = block


def pack(b, first, count, near, me, slot_tile, slot_on, cols, tile):
    _, m_count, n_basis = b.shape
    slots = slot_tile.shape[0]
    rows = tile // cols
    if near:
        out_shape = [jax.ShapeDtypeStruct((slots, count, rows, tile), b.dtype)] * cols
        out_specs = [pl.BlockSpec((slots, 1, rows, tile), lambda p, *_: (0, p, 0, 0))] * cols
    else:
        out_shape = [jax.ShapeDtypeStruct((cols, slots, count, rows, tile), b.dtype)]
        out_specs = [pl.BlockSpec((cols, slots, 1, rows, tile), lambda p, *_: (0, 0, p, 0, 0))]
    return pl.pallas_call(
        functools.partial(pack_kernel, near, slots, tile, n_basis // tile),
        out_shape=out_shape,
        grid_spec=pltpu.PrefetchScalarGridSpec(
            num_scalar_prefetch=3,
            grid=(count,),
            in_specs=[pl.BlockSpec((1, m_count, n_basis), lambda p, *_: (p + first, 0, 0))],
            out_specs=out_specs,
            scratch_shapes=[pltpu.VMEM((m_count, n_basis), jnp.float32)],
        ),
    )(me, slot_tile, slot_on, b)


def lane_block(n_basis, most):
    return min(most, n_basis)


def keep_tiles(mask_ref, first, tile, value_ref, out_ref):
    rows, lanes = out_ref.shape

    @pl.loop(0, rows // tile)
    def _(i):
        down = pl.ds(pl.multiple_of(i * tile, tile), tile)
        for j in range(lanes // tile):
            at = (down, slice(j * tile, (j + 1) * tile))
            kept = value_ref[at]
            out_ref[at] = jnp.where(mask_ref[first + i, j] != 0, kept, jnp.zeros_like(kept))


def mask_kernel(tile, first, mask_ref, value_ref, out_ref):
    keep_tiles(mask_ref, first[0], tile, value_ref, out_ref)


def masked_tiles(value, mask, first, tile):
    return pl.pallas_call(
        functools.partial(mask_kernel, tile),
        out_shape=jax.ShapeDtypeStruct(value.shape, value.dtype),
        grid_spec=pltpu.PrefetchScalarGridSpec(
            num_scalar_prefetch=2,
            grid=(),
            in_specs=[pl.BlockSpec(memory_space=pltpu.VMEM)],
            out_specs=pl.BlockSpec(memory_space=pltpu.VMEM),
        ),
    )(jnp.reshape(first, (1,)), mask, value)


def inner_kernel(tile, starts, sizes, mask_ref, b_ref, virt_ref, *refs):
    out_refs, masked = refs[:-1], refs[-1]
    keep_tiles(mask_ref, 0, tile, b_ref.at[0], masked)
    n_basis = masked.shape[1]
    width = lane_block(n_basis, 512)
    p = pl.program_id(0)

    @pl.loop(0, n_basis // width)
    def _(j):
        lanes = pl.ds(pl.multiple_of(j * width, width), width)
        part = jnp.dot(
            masked[...], virt_ref[:, lanes], preferred_element_type=jnp.float32
        ).astype(masked.dtype)
        for start, size, out_ref in zip(starts, sizes, out_refs):

            @pl.when((p >= start) & (p < start + size))
            def _():
                out_ref[0, :, lanes] = part


def inner(b, first, sizes, mask, virt, tile):
    _, rows, n_basis = b.shape
    starts = [sum(sizes[:i]) for i in range(len(sizes))]
    return pl.pallas_call(
        functools.partial(inner_kernel, tile, starts, sizes),
        out_shape=[jax.ShapeDtypeStruct((size, rows, n_basis), b.dtype) for size in sizes],
        grid_spec=pltpu.PrefetchScalarGridSpec(
            num_scalar_prefetch=1,
            grid=(sum(sizes),),
            in_specs=[
                pl.BlockSpec((1, rows, n_basis), lambda p, mask: (p + first, 0, 0)),
                pl.BlockSpec((n_basis, n_basis), lambda p, mask: (0, 0)),
            ],
            out_specs=[
                pl.BlockSpec(
                    (1, rows, n_basis),
                    lambda p, mask, start=start, size=size: (
                        jnp.clip(p - start, 0, size - 1),
                        0,
                        0,
                    ),
                )
                for start, size in zip(starts, sizes)
            ],
            scratch_shapes=[pltpu.VMEM((rows, n_basis), b.dtype)],
        ),
    )(mask, b, virt)


def outer_kernel(offsets, slots, tile, across, me, slot_tile, occ_ref, *refs):
    half_refs = refs[: len(offsets)]
    out_refs, wide = refs[len(offsets) : -1], refs[-1]
    depth = half_refs[0].shape[1]
    rows = out_refs[0].shape[2]
    width = lane_block(wide.shape[1], 256)

    @pl.loop(0, wide.shape[1] // width)
    def _(j):
        lanes = pl.ds(pl.multiple_of(j * width, width), width)
        total = None
        for offset, half_ref in zip(offsets, half_refs):
            start = pl.multiple_of((me[1] ^ offset) * depth, depth)
            part = jnp.dot(
                occ_ref[:, pl.ds(start, depth)],
                half_ref[0, :, lanes],
                preferred_element_type=jnp.float32,
            )
            total = part if total is None else total + part
        wide[:, lanes] = total

    @pl.loop(0, slots)
    def _(slot):
        top = (slot_tile[slot] // across) * tile
        lane = pl.multiple_of((slot_tile[slot] % across) * tile, tile)
        for k, out_ref in enumerate(out_refs):
            start = pl.multiple_of(top + (me[0] ^ k) * rows, rows)
            block = wide[pl.ds(start, rows), pl.ds(lane, tile)]
            out_ref[slot, 0] = block.astype(out_ref.dtype)


def outer(occ, halves, offsets, me, slot_tile, cols, tile):
    count, depth, n_basis = halves[0].shape
    slots = slot_tile.shape[0]
    strip = (slots, count, tile // cols, tile)
    return pl.pallas_call(
        functools.partial(outer_kernel, offsets, slots, tile, n_basis // tile),
        out_shape=[jax.ShapeDtypeStruct(strip, occ.dtype)] * cols,
        grid_spec=pltpu.PrefetchScalarGridSpec(
            num_scalar_prefetch=2,
            grid=(count,),
            in_specs=[pl.BlockSpec(occ.shape, lambda p, me, which: (0, 0))]
            + [pl.BlockSpec((1, depth, n_basis), lambda p, me, which: (p, 0, 0))] * len(halves),
            out_specs=[
                pl.BlockSpec((slots, 1) + strip[2:], lambda p, me, which: (0, p, 0, 0))
            ]
            * cols,
            scratch_shapes=[pltpu.VMEM((occ.shape[0], n_basis), jnp.float32)],
        ),
    )(me, slot_tile, occ, *halves)


def group_of(slots):
    groups = [size for size in range(2, 9) if slots % size == 0]
    return max(groups, default=slots)


def place(me, strips, slot, wide, base, stride):
    for k, ref in enumerate(strips):
        count = ref.shape[1]
        wide[pl.ds((me[0] ^ k) * stride + base, count)] = ref[slot].astype(jnp.float32)


def unroll_rows(wide, out_ref, start):
    turned = jnp.swapaxes(wide[...], 0, 1).astype(out_ref.dtype)
    rows, _, lanes = turned.shape
    for row in range(rows):
        at = start + row * lanes
        at = at if isinstance(at, int) else pl.multiple_of(at, lanes)
        out_ref[:, pl.ds(at, lanes)] = turned[row]


def flatten_kernel(group, early, me, *refs):
    near_refs, rest_ref, out_ref, wide = refs[:-3], refs[-3], refs[-2], refs[-1]
    cols, _, late, rows, lanes = rest_ref.shape

    @pl.loop(0, group)
    def _(slot):
        place(me, near_refs, slot, wide, 0, early + late)
        for k in range(cols):
            start = k * (early + late) + early
            wide[start : start + late] = rest_ref[k, slot].astype(jnp.float32)
        unroll_rows(wide, out_ref, slot * (rows * lanes))


def flatten(near, rest, me):
    cols, slots, late, rows, lanes = rest.shape
    early = near[0].shape[1]
    total = cols * (early + late)
    group = group_of(slots)
    return pl.pallas_call(
        functools.partial(flatten_kernel, group, early),
        out_shape=jax.ShapeDtypeStruct((total, slots * rows * lanes), rest.dtype),
        grid_spec=pltpu.PrefetchScalarGridSpec(
            num_scalar_prefetch=1,
            grid=(slots // group,),
            in_specs=[pl.BlockSpec((group, early, rows, lanes), lambda s, me: (s, 0, 0, 0))]
            * cols
            + [pl.BlockSpec((cols, group, late, rows, lanes), lambda s, me: (0, s, 0, 0, 0))],
            out_specs=pl.BlockSpec((total, group * rows * lanes), lambda s, me: (0, s)),
            scratch_shapes=[pltpu.VMEM((total, rows, lanes), jnp.float32)],
        ),
    )(me, *near, rest)


def contract_kernel(group, counts, cols, me, *refs):
    strips, b_ref, out_ref, wide, flat = refs[:-4], *refs[-4:]
    width = flat.shape[1]

    @pl.when(pl.program_id(0) == 0)
    def _():
        out_ref[...] = jnp.zeros_like(out_ref)

    @pl.loop(0, group, unroll=1 if group % 2 else 2)
    def _(slot):
        base = 0
        for i, count in enumerate(counts):
            place(me, strips[i * cols : (i + 1) * cols], slot, wide, base, sum(counts))
            base += count
        unroll_rows(wide, flat, 0)
        out_ref[...] += lax.dot_general(
            flat[...],
            b_ref[:, pl.ds(pl.multiple_of(slot * width, width), width)],
            (((1,), (1,)), ((), ())),
            preferred_element_type=jnp.float32,
        )


def contract(chunks, b_flat, me):
    cols = len(chunks[0])
    slots, _, rows, lanes = chunks[0][0].shape
    counts = [chunk[0].shape[1] for chunk in chunks]
    total, width = cols * sum(counts), rows * lanes
    group = group_of(slots)
    return pl.pallas_call(
        functools.partial(contract_kernel, group, counts, cols),
        out_shape=jax.ShapeDtypeStruct((total, b_flat.shape[0]), jnp.float32),
        grid_spec=pltpu.PrefetchScalarGridSpec(
            num_scalar_prefetch=1,
            grid=(slots // group,),
            in_specs=[
                pl.BlockSpec((group, count, rows, lanes), lambda s, me: (s, 0, 0, 0))
                for count in counts
                for _ in range(cols)
            ]
            + [pl.BlockSpec((b_flat.shape[0], group * width), lambda s, me: (0, s))],
            out_specs=pl.BlockSpec((total, b_flat.shape[0]), lambda s, me: (0, 0)),
            scratch_shapes=[
                pltpu.VMEM((total, rows, lanes), jnp.float32),
                pltpu.VMEM((total, width), b_flat.dtype),
            ],
        ),
    )(me, *[strip for chunk in chunks for strip in chunk], b_flat)


def exchange(strips):
    return [strips[0]] + [swap(s, "col", len(strips), k) for k, s in enumerate(strips) if k]


def per_device(row_size, col_size, b_tensor, occ_green, virt_green, b_mask, occ_mask, virt_mask):
    p_count, m_count, n_basis = b_tensor.shape
    tile = n_basis // b_mask.shape[2]
    col_index, row_index = lax.axis_index("col"), lax.axis_index("row")
    me = jnp.stack([col_index, row_index, (col_index * p_count) // tile]).astype(jnp.int32)
    caps = slot_caps(m_count // tile * (n_basis // tile))
    slot_tile, slot_on, branch = plan(b_mask, me, row_size, caps)

    def with_slots(cap, *args):
        return run(row_size, col_size, tile, slot_tile[:cap], slot_on[:cap], me, *args)

    return lax.switch(
        branch[0],
        [functools.partial(with_slots, cap) for cap in caps],
        b_tensor,
        occ_green,
        virt_green,
        b_mask,
        occ_mask,
        virt_mask,
    )


def slot_caps(slots):
    return sorted({slots * part // 16 for part in (13, 14, 16)})


def run(
    row_size,
    col_size,
    tile,
    slot_tile,
    slot_on,
    me,
    b_tensor,
    occ_green,
    virt_green,
    b_mask,
    occ_mask,
    virt_mask,
):
    col_index, row_index = me[0], me[1]
    p_count, m_count, n_basis = b_tensor.shape
    m_tiles = m_count // tile
    across = n_basis // tile
    local_mask = lax.dynamic_slice(b_mask, (me[2], row_index * m_tiles, 0), (1, m_tiles, across))[0]

    green, seen = jnp.stack([virt_green, occ_green]), []
    for bit in xor_bits(col_size):
        upper = (col_index & bit) != 0
        axis = 1 + sum(other > bit for other in seen)
        seen.append(bit)
        green = join(green, swap(green, "col", col_size, bit), upper, axis)
    virt_rows, occ_rows = green.reshape(2, -1, n_basis)

    crowded = slot_tile.shape[0] * 16 >= m_tiles * across * 14
    early = max(1, p_count * (4 if crowded else 3) // 16)
    strips = pack(b_tensor, 0, early, True, me, slot_tile, slot_on, col_size, tile)
    near = exchange(strips)
    (strips,) = pack(
        b_tensor, early, p_count - early, False, me, slot_tile, slot_on, col_size, tile
    )
    rest = lax.all_to_all(strips, "col", split_axis=0, concat_axis=0, tiled=True)

    virt = virt_rows
    for depth, bit in enumerate(xor_bits(row_size)):
        upper = (row_index & bit) != 0
        virt = join(virt, swap(virt, "row", row_size, bit), upper, depth)
    virt = masked_tiles(virt.reshape(n_basis, n_basis), virt_mask, 0, tile)
    occ = masked_tiles(occ_rows, occ_mask, row_index * m_tiles, tile)

    sizes = chunk_sizes(p_count)
    offsets = [0]
    for bit in xor_bits(row_size):
        offsets = offsets + [offset ^ bit for offset in offsets]
    ready = inner(b_tensor, 0, sizes[:1], local_mask, virt, tile)
    ready += inner(b_tensor, sizes[0], sizes[1:], local_mask, virt, tile)
    gathered = []
    for k in range(CHUNKS):
        halves = [ready[k]]
        for bit in xor_bits(row_size):
            halves = halves + [swap(h, "row", row_size, bit) for h in halves]
        gathered.append(halves)
    moved = []
    for k in range(CHUNKS):
        strips = outer(occ, gathered[k], offsets, me, slot_tile, col_size, tile)
        moved.append(exchange(strips))

    b_flat = flatten(near, rest, me)
    sums = []
    sums.append(contract(moved[:-1], b_flat, me))
    sums.append(contract(moved[-1:], b_flat, me))
    sums = [part.reshape(col_size, -1, part.shape[-1]) for part in sums]
    total = jnp.concatenate(sums, axis=1)
    total = total.reshape(row_size * col_size, -1, total.shape[-1])
    shares = lax.all_to_all(total, ("row", "col"), split_axis=0, concat_axis=0, tiled=True)
    return shares.sum(0) * (-2.0 / n_basis)


def solution(mesh):
    row_size, col_size = mesh.shape["row"], mesh.shape["col"]

    return jax.shard_map(
        functools.partial(per_device, row_size, col_size),
        mesh=mesh,
        in_specs=(
            P("col", "row", None),
            P(("row", "col"), None),
            P(("row", "col"), None),
            P(),
            P(),
            P(),
        ),
        out_specs=P(("row", "col"), None),
        check_vma=False,
    )
```
